256 devices in a mesh: region: 32 (over z, x), eig: 8 (over y, core).
Axes of the slice: x: 4, y: 4, z: 8, core: 2. Of those that a mesh axis runs over, the one named last changes fastest.
Arguments:
- residual: float32 [2, 768, 32, 3072], P(None, 'region', None, 'eig'), may hold values from -6 to 6
- basis: float32 [2, 768, 64, 3072], P(None, 'region', None, 'eig'), may hold values from -0.078125 to 0.078125
- eigvecs: bfloat16 [2, 768, 64, 1024], P(None, 'region', None, 'eig'), may hold values from -0.01953125 to 0.01953125
- weights: float32 [1024], P('eig'), may hold values from 24 to 96
Outputs:
- correction: float32 [2, 768, 32, 3072], P(None, 'region', None, 'eig')
The draws below stay inside these ranges and needn't reach their ends.
All inputs are finite; a program needn't handle non-finite values.
Results may differ from the reference program's by a relative error of at most 0.013.
Values may be sent and summed in bfloat16 or wider, within the bound.
A program may use at most 64 MiB of HBM per device.

```python
import math
import jax
import jax.numpy as jnp
from jax import lax

COMP = 3072
BASIS = 64
EIGVEC = 1024
COLS = 32
BLOCKS = 768


def level_of(rng, extent, split, smallest, largest):
    factor_of = 1.0
    for dim, shards_of in split:
        steps = jax.random.uniform(jax.random.fold_in(jax.random.fold_in(rng, 6), dim), (shards_of,), jnp.float32, smallest / len(split), largest / len(split))
        factor_of = factor_of * jnp.repeat(jnp.exp(steps), extent[dim] // shards_of).reshape((-1,) + (1,) * (len(extent) - 1 - dim))
    return factor_of


def bell_draw(key, shape, scale, limit, shards=(), held_as=jnp.bfloat16):
    array = scale * jax.random.normal(key, shape, jnp.float32)
    if shards:
        array = array * level_of(key, shape, shards, -0.22, 0.18)
    return jnp.clip(array, -limit, limit).astype(held_as)


def setup_inputs(seed: int = 0) -> dict:
    splits = jax.random.split(jax.random.key(seed), 5)
    return {
        "residual": bell_draw(splits[0], (2, BLOCKS, COLS, COMP), 1.0, 6.0, ((1, 32), (3, 8)), jnp.float32),
        "basis": bell_draw(splits[1], (2, BLOCKS, BASIS, COMP), (2 * COMP) ** -0.5, 0.078125, ((1, 32), (3, 8)), jnp.float32),
        "eigvecs": bell_draw(splits[2], (2, BLOCKS, BASIS, EIGVEC), (2 * BASIS * BLOCKS) ** -0.5, 0.01953125, ((1, 32), (3, 8))),
        "weights": jnp.clip(jnp.exp(math.log(96.0) - 1.3862944 * jax.random.uniform(splits[3], (EIGVEC,), jnp.float32) ** level_of(splits[3], (EIGVEC,), ((0, 8),), -0.2, 0.2)), 24.0, 96.0),
    }


def mix(form, left, right):
    return jnp.einsum(form, left, right, precision=lax.Precision.HIGHEST)


def mix_low(form, left, right):
    return jnp.einsum(form, left.astype(jnp.float32), right.astype(jnp.float32))


def reference(residual, basis, eigvecs, weights):
    res_re, res_im = residual[0], residual[1]
    bas_re, bas_im = basis[0], basis[1]
    eig_re, eig_im = eigvecs[0], eigvecs[1]
    coarse_re = mix("bkc,bnc->bnk", bas_re, res_re) + mix("bkc,bnc->bnk", bas_im, res_im)
    coarse_im = mix("bkc,bnc->bnk", bas_re, res_im) - mix("bkc,bnc->bnk", bas_im, res_re)
    coarse_re = coarse_re.astype(jnp.bfloat16)
    coarse_im = coarse_im.astype(jnp.bfloat16)
    spec_re = mix_low("bnk,bkj->nj", coarse_re, eig_re) + mix_low("bnk,bkj->nj", coarse_im, eig_im)
    spec_im = mix_low("bnk,bkj->nj", coarse_im, eig_re) - mix_low("bnk,bkj->nj", coarse_re, eig_im)
    wgt_re = (spec_re * weights[None, :]).astype(jnp.bfloat16)
    wgt_im = (spec_im * weights[None, :]).astype(jnp.bfloat16)
    lift_re = mix_low("nj,bkj->bnk", wgt_re, eig_re) - mix_low("nj,bkj->bnk", wgt_im, eig_im)
    lift_im = mix_low("nj,bkj->bnk", wgt_re, eig_im) + mix_low("nj,bkj->bnk", wgt_im, eig_re)
    out_re = mix("bkc,bnk->bnc", bas_re, lift_re) - mix("bkc,bnk->bnc", bas_im, lift_im)
    out_im = mix("bkc,bnk->bnc", bas_re, lift_im) + mix("bkc,bnk->bnc", bas_im, lift_re)
    return jnp.stack([out_re, out_im])
```

```python
import functools

import jax
import jax.numpy as jnp
from jax import lax
from jax.experimental import pallas as pl
from jax.experimental.pallas import tpu as pltpu
from jax.sharding import PartitionSpec as P

MESH = pl.DeviceIdType.MESH
BF16 = jnp.bfloat16
F32 = jnp.float32

BLOCKS = 24
COLS = 32
BASIS = 64
COMP = 384
EIGV = 128
SHARE = 8
CHUNKS = BLOCKS // SHARE
X, Y, Z = 4, 4, 8
GROUP = 4
FAR_FIRST = ((2, 0), (2, 1), (1, 0), (1, 1), (3, 0), (3, 1), (0, 1))
Z_FAR_FIRST = (4, 3, 5, 2, 6, 1, 7)
X_FAR_FIRST = (2, 1, 3)


def signs(rows):
    lane = lax.broadcasted_iota(jnp.int32, (rows, 2 * BASIS), 1)
    return jnp.where(lane < BASIS, 1.0, -1.0).astype(F32)


def coefficients(
    res,
    bas,
    eig,
    wts,
    bas_out,
    lift_out,
    rv,
    bv,
    ev,
    wv,
    part,
    part_in,
    coarse,
    lpart,
    lpart_in,
    lift,
    spec,
    spec_in,
    zown,
    zin,
    wall,
    load_sem,
    eig_sem,
    rs_send,
    rs_recv,
    ag_send,
    ag_recv,
    x_send,
    x_recv,
    z_send,
    z_recv,
    w_send,
    w_recv,
):
    region = lax.axis_index("region")
    me = lax.axis_index("eig")
    x, z = lax.rem(region, X), lax.div(region, X)
    core, y = lax.rem(me, 2), lax.div(me, 2)

    loads = []
    for g in range(BLOCKS // GROUP):
        span = pl.ds(g * GROUP, GROUP)
        pair = (
            pltpu.make_async_copy(bas.at[:, span], bv.at[:, span], load_sem.at[0, g]),
            pltpu.make_async_copy(res.at[:, span], rv.at[:, span], load_sem.at[1, g]),
        )
        for copy in pair:
            copy.start()
        loads.append(pair)
    eig_load = pltpu.make_async_copy(eig, ev, eig_sem)
    eig_load.start()

    def eig_peer(dy, dc):
        return (region, lax.rem(y + dy, Y) * 2 + lax.rem(core + dc, 2))

    def x_peer(dx):
        return (z * X + lax.rem(x + dx, X), me)

    def z_peer(dz):
        return (lax.rem(z + dz, Z) * X + x, me)

    peers = [eig_peer(*d) for d in FAR_FIRST]
    peers += [x_peer(d) for d in X_FAR_FIRST] + [z_peer(d) for d in Z_FAR_FIRST]
    barrier = pltpu.get_barrier_semaphore()
    for peer in peers:
        pl.semaphore_signal(barrier, inc=1, device_id=peer, device_id_type=MESH)

    sent = []

    def send(src, dst, send_sem, recv_sem, peer):
        copy = pltpu.make_async_remote_copy(
            src_ref=src,
            dst_ref=dst,
            send_sem=send_sem,
            recv_sem=recv_sem,
            device_id=peer,
            device_id_type=MESH,
        )
        copy.start()
        sent.append(copy)
        return copy

    def scatter(which, c, own, inbox):
        copies = []
        for i, d in enumerate(FAR_FIRST):
            peer = eig_peer(*d)
            copies.append(
                send(
                    own.at[SHARE * c + peer[1]],
                    inbox.at[c, i],
                    rs_send.at[which, c, i],
                    rs_recv.at[which, c, i],
                    peer,
                )
            )
        return copies

    def gather(which, c, copies, own, inbox, whole):
        mine = SHARE * c + me
        total = own[mine].astype(F32)
        for i in reversed(range(len(FAR_FIRST))):
            copies[i].wait_recv()
            total += inbox[c, i].astype(F32)
        whole[mine] = total.astype(BF16)
        out = []
        for i, d in enumerate(FAR_FIRST):
            out.append(
                send(
                    whole.at[mine],
                    whole.at[mine],
                    ag_send.at[which, c, i],
                    ag_recv.at[which, c, i],
                    eig_peer(*d),
                )
            )
        return out

    sign = signs(COLS)

    def project(b):
        r = jnp.concatenate([rv[0, b], rv[1, b]], 0).astype(BF16)
        k = jnp.concatenate([bv[0, b], bv[1, b]], 0).astype(BF16)
        bas_out[b] = k
        p = lax.dot_general(r, k, (((1,), (1,)), ((), ())), preferred_element_type=F32)
        part[b] = (p[:COLS] * sign + pltpu.roll(p[COLS:], BASIS, 1)).astype(BF16)

    rs = []
    for c in range(CHUNKS):
        for g in range(c * SHARE // GROUP, (c + 1) * SHARE // GROUP):
            for copy in loads[g]:
                copy.wait()
            for b in range(g * GROUP, (g + 1) * GROUP):
                project(b)
        if c == 0:
            pl.semaphore_wait(barrier, len(peers))
        rs.append(scatter(0, c, part, part_in))

    eig_load.wait()
    for b in range(BLOCKS):
        re, im = ev[0, b], ev[1, b]
        wv[b, :BASIS, :EIGV] = re
        wv[b, :BASIS, EIGV:] = -im
        wv[b, BASIS:, :EIGV] = im
        wv[b, BASIS:, EIGV:] = re

    ag = [gather(0, c, rs[c], part, part_in, coarse) for c in range(CHUNKS)]
    total = jnp.zeros((COLS, 2 * EIGV), F32)
    for c in range(CHUNKS):
        for copy in ag[c]:
            copy.wait_recv()
        for b in range(SHARE * c, SHARE * (c + 1)):
            total += jnp.dot(coarse[b], wv[b], preferred_element_type=F32)

    half = COLS // 2
    for q in range(X):
        row, col = half * (q // 2), EIGV * (q % 2)
        spec[q] = total[row : row + half, col : col + EIGV].astype(BF16)
    xs = [
        send(spec.at[x_peer(d)[0] - z * X], spec_in.at[i], x_send.at[i], x_recv.at[i], x_peer(d))
        for i, d in enumerate(X_FAR_FIRST)
    ]
    quarter = spec[x].astype(F32)
    for i in reversed(range(len(xs))):
        xs[i].wait_recv()
        quarter += spec_in[i].astype(F32)
    zown[...] = quarter.astype(BF16)
    zs = [
        send(zown, zin.at[i], z_send.at[i], z_recv.at[i], z_peer(d))
        for i, d in enumerate(Z_FAR_FIRST)
    ]
    for i in reversed(range(len(zs))):
        zs[i].wait_recv()
        quarter += zin[i].astype(F32)
    wall[x] = (quarter * wts[...]).astype(BF16)
    ws = [
        send(wall.at[x], wall.at[x], w_send.at[i], w_recv.at[i], x_peer(d))
        for i, d in enumerate(X_FAR_FIRST)
    ]
    for copy in ws:
        copy.wait_recv()
    weighted = jnp.concatenate(
        [
            jnp.concatenate([wall[0], wall[1]], 1),
            jnp.concatenate([wall[2], wall[3]], 1),
        ],
        0,
    )

    rs = []
    for c in range(CHUNKS):
        for b in range(SHARE * c, SHARE * (c + 1)):
            lpart[b] = lax.dot_general(
                weighted, wv[b], (((1,), (1,)), ((), ())), preferred_element_type=F32
            ).astype(BF16)
        rs.append(scatter(1, c, lpart, lpart_in))
    ag = [gather(1, c, rs[c], lpart, lpart_in, lift) for c in range(CHUNKS)]
    for c in range(CHUNKS):
        for copy in ag[c]:
            copy.wait_recv()
        for b in range(SHARE * c, SHARE * (c + 1)):
            lift_out[b] = lift[b]
    for copy in sent:
        copy.wait_send()


def prolong(lift, bas, out):
    sign = signs(COLS)
    for b in range(lift.shape[0]):
        l = lift[b].astype(F32)
        rows = jnp.concatenate([l * sign, pltpu.roll(l, BASIS, 1)], 0).astype(BF16)
        both = jnp.dot(rows, bas[b], preferred_element_type=F32)
        out[0, b] = both[:COLS]
        out[1, b] = both[COLS:]


def shards(residual, basis, eigvecs, weights):
    any_spec = pl.BlockSpec(memory_space=pl.ANY)
    vmem_spec = pl.BlockSpec(memory_space=pltpu.VMEM)
    sem = pltpu.SemaphoreType.DMA
    n = len(FAR_FIRST)
    block = (COLS, 2 * BASIS)
    bas, lift = pl.pallas_call(
        coefficients,
        out_shape=(
            jax.ShapeDtypeStruct((BLOCKS, 2 * BASIS, COMP), BF16),
            jax.ShapeDtypeStruct((BLOCKS, *block), BF16),
        ),
        in_specs=[any_spec, any_spec, any_spec, vmem_spec],
        out_specs=(vmem_spec, vmem_spec),
        scratch_shapes=[
            pltpu.VMEM((2, BLOCKS, COLS, COMP), F32),
            pltpu.VMEM((2, BLOCKS, BASIS, COMP), F32),
            pltpu.VMEM((2, BLOCKS, BASIS, EIGV), BF16),
            pltpu.VMEM((BLOCKS, 2 * BASIS, 2 * EIGV), BF16),
            pltpu.VMEM((BLOCKS, *block), BF16),
            pltpu.VMEM((CHUNKS, n, *block), BF16),
            pltpu.VMEM((BLOCKS, *block), BF16),
            pltpu.VMEM((BLOCKS, *block), BF16),
            pltpu.VMEM((CHUNKS, n, *block), BF16),
            pltpu.VMEM((BLOCKS, *block), BF16),
            pltpu.VMEM((X, COLS // 2, EIGV), BF16),
            pltpu.VMEM((X - 1, COLS // 2, EIGV), BF16),
            pltpu.VMEM((COLS // 2, EIGV), BF16),
            pltpu.VMEM((Z - 1, COLS // 2, EIGV), BF16),
            pltpu.VMEM((X, COLS // 2, EIGV), BF16),
            sem((2, BLOCKS // GROUP)),
            sem,
            sem((2, CHUNKS, n)),
            sem((2, CHUNKS, n)),
            sem((2, CHUNKS, n)),
            sem((2, CHUNKS, n)),
            sem((X - 1,)),
            sem((X - 1,)),
            sem((Z - 1,)),
            sem((Z - 1,)),
            sem((X - 1,)),
            sem((X - 1,)),
        ],
        compiler_params=pltpu.CompilerParams(
            collective_id=0, has_side_effects=True, vmem_limit_bytes=24 << 20
        ),
    )(residual, basis, eigvecs, weights.reshape(1, EIGV))

    step = 4
    return pl.pallas_call(
        prolong,
        grid=(BLOCKS // step,),
        out_shape=jax.ShapeDtypeStruct((2, BLOCKS, COLS, COMP), F32),
        in_specs=[
            pl.BlockSpec((step, *block), lambda i: (i, 0, 0)),
            pl.BlockSpec((step, 2 * BASIS, COMP), lambda i: (i, 0, 0)),
        ],
        out_specs=pl.BlockSpec((2, step, COLS, COMP), lambda i: (0, i, 0, 0)),
        compiler_params=pltpu.CompilerParams(vmem_limit_bytes=16 << 20),
    )(lift, bas)


def solution(mesh):
    in_specs = (
        P(None, "region", None, "eig"),
        P(None, "region", None, "eig"),
        P(None, "region", None, "eig"),
        P("eig"),
    )
    out_specs = P(None, "region", None, "eig")
    return jax.shard_map(shards, mesh=mesh, in_specs=in_specs, out_specs=out_specs, check_vma=False)
```

```python
import functools

import jax
import jax.numpy as jnp
from jax import lax
from jax.experimental import pallas as pl
from jax.experimental.pallas import tpu as pltpu
from jax.sharding import PartitionSpec as P

MESH = pl.DeviceIdType.MESH
BF16 = jnp.bfloat16
F32 = jnp.float32

BLOCKS = 24
COLS = 32
BASIS = 64
COMP = 384
EIGV = 128
X, Y, Z = 4, 4, 8
CHUNK = 8
HALF = CHUNK // 2
CHUNKS = BLOCKS // CHUNK
GROUP = 4
ALONG_X = (2, 1, 3)
ALONG_Y = (2, 1, 3)
ALONG_Z = (4, 3, 5, 2, 6, 1, 7)


def signs(rows):
    lane = lax.broadcasted_iota(jnp.int32, (rows, 2 * BASIS), 1)
    return jnp.where(lane < BASIS, 1.0, -1.0).astype(F32)


def coefficients(
    res,
    bas,
    eig,
    wts,
    bas_out,
    lift_out,
    rv,
    bv,
    ev,
    wtv,
    wv,
    part,
    core_in,
    chip,
    chip_in,
    whole,
    spec,
    spec_in,
    zown,
    zin,
    load_sem,
    eig_sem,
    c_send,
    c_recv,
    y_send,
    y_recv,
    g_send,
    g_recv,
    x_send,
    x_recv,
    z_send,
    z_recv,
):
    region = lax.axis_index("region")
    me = lax.axis_index("eig")
    x, z = lax.rem(region, X), lax.div(region, X)
    core, y = lax.rem(me, 2), lax.div(me, 2)

    loads = []
    for g in range(BLOCKS // GROUP):
        span = pl.ds(g * GROUP, GROUP)
        pair = (
            pltpu.make_async_copy(bas.at[:, span], bv.at[:, span], load_sem.at[0, g]),
            pltpu.make_async_copy(res.at[:, span], rv.at[:, span], load_sem.at[1, g]),
        )
        for copy in pair:
            copy.start()
        loads.append(pair)
    eig_load = pltpu.make_async_copy(eig, ev, eig_sem.at[0])
    wts_load = pltpu.make_async_copy(wts, wtv, eig_sem.at[1])
    eig_load.start()
    wts_load.start()

    partner = (region, y * 2 + 1 - core)
    x_peers = [(z * X + lax.rem(x + d, X), me) for d in ALONG_X]
    y_peers = [(region, lax.rem(y + d, Y) * 2 + core) for d in ALONG_Y]
    z_peers = [(lax.rem(z + d, Z) * X + x, me) for d in ALONG_Z]
    peers = [partner] + x_peers + y_peers + z_peers
    barrier = pltpu.get_barrier_semaphore()
    for peer in peers:
        pl.semaphore_signal(barrier, inc=1, device_id=peer, device_id_type=MESH)

    sent = []

    def send(src, dst, send_sem, recv_sem, peer):
        copy = pltpu.make_async_remote_copy(
            src_ref=src,
            dst_ref=dst,
            send_sem=send_sem,
            recv_sem=recv_sem,
            device_id=peer,
            device_id_type=MESH,
        )
        copy.start()
        sent.append(copy)
        return copy

    def mine(c):
        return pl.ds(CHUNK * c + HALF * core, HALF)

    def to_partner(w, c):
        theirs = pl.ds(CHUNK * c + HALF * (1 - core), HALF)
        return send(
            part.at[w, theirs], core_in.at[w, c], c_send.at[w, c], c_recv.at[w, c], partner
        )

    def along_y(w, c, copy):
        copy.wait_recv()
        total = part[w, mine(c)].astype(F32) + core_in[w, c].astype(F32)
        chip[w, c] = total.astype(BF16)
        return [
            send(chip.at[w, c], chip_in.at[w, c, i], y_send.at[w, c, i], y_recv.at[w, c, i], peer)
            for i, peer in enumerate(y_peers)
        ]

    def to_chip(w, c, copies):
        total = chip[w, c].astype(F32)
        for i in (1, 2, 0):
            copies[i].wait_recv()
            total += chip_in[w, c, i].astype(F32)
        whole[w, mine(c)] = total.astype(BF16)
        done = whole.at[w, mine(c)]
        return send(done, done, g_send.at[w, c], g_recv.at[w, c], partner)

    def exchange(w, produce, between, consume):
        pair, over_y, over_chip = {}, {}, {}
        for c in range(CHUNKS):
            produce(c)
            if w == 0 and c == 0:
                pl.semaphore_wait(barrier, len(peers))
            pair[c] = to_partner(w, c)
            if c > 0:
                over_y[c - 1] = along_y(w, c - 1, pair[c - 1])
        between()
        over_y[CHUNKS - 1] = along_y(w, CHUNKS - 1, pair[CHUNKS - 1])
        for c in range(CHUNKS):
            over_chip[c] = to_chip(w, c, over_y[c])
            if c > 0:
                over_chip[c - 1].wait_recv()
                consume(c - 1)
        over_chip[CHUNKS - 1].wait_recv()
        consume(CHUNKS - 1)

    def blocks_of(c):
        return range(CHUNK * c, CHUNK * (c + 1))

    sign = signs(COLS)

    def project(c):
        for g in range(c * CHUNK // GROUP, (c + 1) * CHUNK // GROUP):
            for copy in loads[g]:
                copy.wait()
            for b in range(g * GROUP, (g + 1) * GROUP):
                r = jnp.concatenate([rv[0, b], rv[1, b]], 0).astype(BF16)
                k = jnp.concatenate([bv[0, b], bv[1, b]], 0).astype(BF16)
                bas_out[b] = k
                p = lax.dot_general(r, k, (((1,), (1,)), ((), ())), preferred_element_type=F32)
                part[0, b] = (p[:COLS] * sign + pltpu.roll(p[COLS:], BASIS, 1)).astype(BF16)

    def pack():
        eig_load.wait()
        wts_load.wait()
        for b in range(BLOCKS):
            re, im = ev[0, b], ev[1, b]
            wv[b, :BASIS, :EIGV] = re
            wv[b, :BASIS, EIGV:] = -im
            wv[b, BASIS:, :EIGV] = im
            wv[b, BASIS:, EIGV:] = re

    sums = []

    def contract(c):
        total = sums.pop() if sums else jnp.zeros((COLS, 2 * EIGV), F32)
        for b in blocks_of(c):
            total += jnp.dot(whole[0, b], wv[b], preferred_element_type=F32)
        sums.append(total)

    exchange(0, project, pack, contract)

    total = sums.pop()
    spec[...] = total.astype(BF16)
    xs = [
        send(spec, spec_in.at[i], x_send.at[i], x_recv.at[i], peer)
        for i, peer in enumerate(x_peers)
    ]
    for i in reversed(range(len(xs))):
        xs[i].wait_recv()
        total += spec_in[i].astype(F32)
    zown[...] = total.astype(BF16)
    zs = [
        send(zown, zin.at[i], z_send.at[i], z_recv.at[i], peer) for i, peer in enumerate(z_peers)
    ]
    for i in reversed(range(len(zs))):
        zs[i].wait_recv()
        total += zin[i].astype(F32)
    weighted = (total * jnp.concatenate([wtv[...], wtv[...]], 1)).astype(BF16)

    def expand(c):
        for b in blocks_of(c):
            part[1, b] = lax.dot_general(
                weighted, wv[b], (((1,), (1,)), ((), ())), preferred_element_type=F32
            ).astype(BF16)

    def hand_on(c):
        for b in blocks_of(c):
            lift_out[b] = whole[1, b]

    exchange(1, expand, lambda: None, hand_on)
    for copy in sent:
        copy.wait_send()


def prolong(lift, bas, out, ov, sem):
    sign = signs(COLS)
    copies = []
    for c in range(CHUNKS):
        for b in range(CHUNK * c, CHUNK * (c + 1)):
            l = lift[b].astype(F32)
            rows = jnp.concatenate([l * sign, pltpu.roll(l, BASIS, 1)], 0).astype(BF16)
            both = jnp.dot(rows, bas[b], preferred_element_type=F32)
            ov[0, b] = both[:COLS]
            ov[1, b] = both[COLS:]
        span = pl.ds(CHUNK * c, CHUNK)
        copies.append(pltpu.make_async_copy(ov.at[:, span], out.at[:, span], sem.at[c]))
        copies[-1].start()
    for copy in copies:
        copy.wait()


def shards(residual, basis, eigvecs, weights):
    hbm_spec = pl.BlockSpec(memory_space=pltpu.HBM)
    vmem_spec = pl.BlockSpec(memory_space=pltpu.VMEM)
    sem = pltpu.SemaphoreType.DMA
    block = (COLS, 2 * BASIS)
    spectral = (COLS, 2 * EIGV)
    args = [
        pltpu.with_memory_space_constraint(a, pltpu.HBM)
        for a in (residual, basis, eigvecs, weights.reshape(1, EIGV))
    ]
    bas, lift = pl.pallas_call(
        coefficients,
        out_shape=(
            jax.ShapeDtypeStruct((BLOCKS, 2 * BASIS, COMP), BF16),
            jax.ShapeDtypeStruct((BLOCKS, *block), BF16),
        ),
        in_specs=[hbm_spec] * 4,
        out_specs=(vmem_spec, vmem_spec),
        scratch_shapes=[
            pltpu.VMEM((2, BLOCKS, COLS, COMP), F32),
            pltpu.VMEM((2, BLOCKS, BASIS, COMP), F32),
            pltpu.VMEM((2, BLOCKS, BASIS, EIGV), BF16),
            pltpu.VMEM((1, EIGV), F32),
            pltpu.VMEM((BLOCKS, 2 * BASIS, 2 * EIGV), BF16),
            pltpu.VMEM((2, BLOCKS, *block), BF16),
            pltpu.VMEM((2, CHUNKS, HALF, *block), BF16),
            pltpu.VMEM((2, CHUNKS, HALF, *block), BF16),
            pltpu.VMEM((2, CHUNKS, Y - 1, HALF, *block), BF16),
            pltpu.VMEM((2, BLOCKS, *block), BF16),
            pltpu.VMEM(spectral, BF16),
            pltpu.VMEM((X - 1, *spectral), BF16),
            pltpu.VMEM(spectral, BF16),
            pltpu.VMEM((Z - 1, *spectral), BF16),
            sem((2, BLOCKS // GROUP)),
            sem((2,)),
            sem((2, CHUNKS)),
            sem((2, CHUNKS)),
            sem((2, CHUNKS, Y - 1)),
            sem((2, CHUNKS, Y - 1)),
            sem((2, CHUNKS)),
            sem((2, CHUNKS)),
            sem((X - 1,)),
            sem((X - 1,)),
            sem((Z - 1,)),
            sem((Z - 1,)),
        ],
        compiler_params=pltpu.CompilerParams(
            collective_id=0, has_side_effects=True, vmem_limit_bytes=24 << 20
        ),
    )(*args)

    return pl.pallas_call(
        prolong,
        out_shape=jax.ShapeDtypeStruct((2, BLOCKS, COLS, COMP), F32),
        in_specs=[vmem_spec, vmem_spec],
        out_specs=hbm_spec,
        scratch_shapes=[pltpu.VMEM((2, BLOCKS, COLS, COMP), F32), sem((CHUNKS,))],
        compiler_params=pltpu.CompilerParams(vmem_limit_bytes=16 << 20),
    )(lift, bas)


def solution(mesh):
    in_specs = (
        P(None, "region", None, "eig"),
        P(None, "region", None, "eig"),
        P(None, "region", None, "eig"),
        P("eig"),
    )
    out_specs = P(None, "region", None, "eig")
    return jax.shard_map(shards, mesh=mesh, in_specs=in_specs, out_specs=out_specs, check_vma=False)
```

```python
import functools

import jax
import jax.numpy as jnp
from jax import lax
from jax.experimental import pallas as pl
from jax.experimental.pallas import tpu as pltpu
from jax.sharding import PartitionSpec as P

MESH = pl.DeviceIdType.MESH
BF16 = jnp.bfloat16
F32 = jnp.float32

BLOCKS = 24
COLS = 32
BASIS = 64
COMP = 384
EIGV = 128
X, Y, Z = 4, 4, 8
CHUNK = 4
HALF = CHUNK // 2
CHUNKS = BLOCKS // CHUNK
LAG = 2
GROUP = 4
ALONG_X = (2, 1, 3)
ALONG_Y = (2, 1, 3)
ALONG_Z = (4, 3, 5, 2, 6, 1, 7)
ALONG_X_CORE = ((2, 0), (2, 1), (1, 0), (1, 1), (3, 0), (3, 1), (0, 1))


def signs(rows):
    lane = lax.broadcasted_iota(jnp.int32, (rows, 2 * BASIS), 1)
    return jnp.where(lane < BASIS, 1.0, -1.0).astype(F32)


def coefficients(
    res,
    bas,
    eig,
    wts,
    out,
    loaded,
    basis,
    ev,
    ev_in,
    wtv,
    wv,
    wv_in,
    part,
    core_in,
    chip,
    chip_in,
    whole,
    spec,
    spec_in,
    zown,
    zin,
    load_sem,
    eig_sem,
    e_send,
    e_recv,
    c_send,
    c_recv,
    y_send,
    y_recv,
    g_send,
    g_recv,
    x_send,
    x_recv,
    z_send,
    z_recv,
    met,
):
    region = lax.axis_index("region")
    me = lax.axis_index("eig")
    x, z = lax.rem(region, X), lax.div(region, X)
    core, y = lax.rem(me, 2), lax.div(me, 2)

    partner = (region, y * 2 + 1 - core)
    x_peers = [
        (z * X + lax.rem(x + d, X), y * 2 + lax.rem(core + dc, 2)) for d, dc in ALONG_X_CORE
    ]
    y_peers = [(region, lax.rem(y + d, Y) * 2 + core) for d in ALONG_Y]
    z_peers = [(lax.rem(z + d, Z) * X + x, me) for d in ALONG_Z]
    barrier = pltpu.get_barrier_semaphore()

    def greet(sem, peer):
        pl.semaphore_signal(sem, inc=1, device_id=peer, device_id_type=MESH)

    for d in ALONG_Z:
        greet(barrier, (lax.rem(z + d, Z) * X + x, y * 2 + 1))
    for d in ALONG_X:
        greet(barrier, (z * X + lax.rem(x + d, X), y * 2 + 1))
    for d in ALONG_Y:
        greet(barrier, (region, lax.rem(y + d, Y) * 2))
    greet(barrier, partner)

    loads = []
    for g in range(BLOCKS // GROUP):
        span = pl.ds(g * GROUP, GROUP)
        into = loaded.at[:, span]
        pltpu.make_async_copy(bas.at[:, span], into.at[:, :, COLS:], load_sem.at[g]).start()
        pltpu.make_async_copy(res.at[:, span], into.at[:, :, :COLS], load_sem.at[g]).start()
        loads.append(into)
    eig_load = pltpu.make_async_copy(eig, ev, eig_sem.at[0])
    wts_load = pltpu.make_async_copy(wts, wtv, eig_sem.at[1])
    eig_load.start()
    wts_load.start()

    def meet_chips(counter, others):
        @pl.when(core == counter)
        def _():
            pl.semaphore_wait(barrier, others)
            greet(met, partner)

        @pl.when(core != counter)
        def _():
            pl.semaphore_wait(met, 1)

    def arrived(ref, sem):
        pltpu.make_async_copy(ref, ref, sem).wait()

    def send(src, dst, send_sem, recv_sem, peer):
        pltpu.make_async_remote_copy(
            src_ref=src,
            dst_ref=dst,
            send_sem=send_sem,
            recv_sem=recv_sem,
            device_id=peer,
            device_id_type=MESH,
        ).start()

    def mine(c):
        return pl.ds(CHUNK * c + HALF * core, HALF)

    def to_partner(w, c):
        theirs = pl.ds(CHUNK * c + HALF * (1 - core), HALF)
        send(part.at[w, theirs], core_in.at[w, c], c_send, c_recv.at[w, c], partner)

    def along_y(w, c):
        arrived(core_in.at[w, c], c_recv.at[w, c])
        total = part[w, mine(c)].astype(F32) + core_in[w, c].astype(F32)
        chip[w, c] = total.astype(BF16)
        for i, peer in enumerate(y_peers):
            send(chip.at[w, c], chip_in.at[w, c, i], y_send, y_recv.at[w, c], peer)

    def over_y(w, c):
        arrived(chip_in.at[w, c], y_recv.at[w, c])
        total = chip[w, c].astype(F32)
        for i in range(len(y_peers)):
            total += chip_in[w, c, i].astype(F32)
        return total.astype(BF16)

    def blocks_of(c):
        return range(CHUNK * c, CHUNK * (c + 1))

    sign = signs(COLS)

    def project(c):
        for g in range(c * CHUNK // GROUP, (c + 1) * CHUNK // GROUP):
            arrived(loads[g], load_sem.at[g])
            for b in range(g * GROUP, (g + 1) * GROUP):
                r = jnp.concatenate([loaded[0, b, :COLS], loaded[1, b, :COLS]], 0).astype(BF16)
                k = jnp.concatenate([loaded[0, b, COLS:], loaded[1, b, COLS:]], 0).astype(BF16)
                basis[b] = k
                p = lax.dot_general(r, k, (((1,), (1,)), ((), ())), preferred_element_type=F32)
                part[0, b] = (p[:COLS] * sign + pltpu.roll(p[COLS:], BASIS, 1)).astype(BF16)

    def as_real(to, re, im):
        to[:BASIS, :EIGV] = re
        to[:BASIS, EIGV:] = -im
        to[BASIS:, :EIGV] = im
        to[BASIS:, EIGV:] = re

    def swap():
        eig_load.wait()
        for c in range(CHUNKS):
            theirs = pl.ds(CHUNK * c + HALF * (1 - core), HALF)
            send(ev.at[:, theirs], ev_in.at[:, c], e_send, e_recv, partner)

    for c in range(CHUNKS):
        project(c)
        if c == 0:
            meet_chips(0, 2 * (Y - 1) + 1)
        to_partner(0, c)
        if c >= LAG:
            along_y(0, c - LAG)
    swap()
    for c in range(CHUNKS - LAG, CHUNKS):
        along_y(0, c)
    for b in range(BLOCKS):
        as_real(wv.at[b], ev[0, b], ev[1, b])
    arrived(ev_in, e_recv)
    for c in range(CHUNKS):
        for i in range(HALF):
            as_real(wv_in.at[c, i], ev_in[0, c, i], ev_in[1, c, i])
    wts_load.wait()
    meet_chips(1, 2 * (X - 1) + 2 * (Z - 1) + 1)
    total = jnp.zeros((COLS, 2 * EIGV), F32)
    other = jnp.zeros((COLS, 2 * EIGV), F32)
    for c in range(CHUNKS):
        half = over_y(0, c)
        for i in range(HALF):
            total += jnp.dot(
                half[i], wv[CHUNK * c + HALF * core + i], preferred_element_type=F32
            )
            other += jnp.dot(half[i], wv_in[c, i], preferred_element_type=F32)

    spec[0] = total.astype(BF16)
    spec[1] = other.astype(BF16)
    for i, (d, peer) in enumerate(zip(ALONG_X_CORE, x_peers)):
        send(spec.at[d[1]], spec_in.at[i], x_send, x_recv, peer)
    arrived(spec_in, x_recv)
    for i in range(len(x_peers)):
        total += spec_in[i].astype(F32)
    zown[...] = total.astype(BF16)
    for i, peer in enumerate(z_peers):
        send(zown, zin.at[i], z_send, z_recv, peer)
    arrived(zin, z_recv)
    for i in range(len(z_peers)):
        total += zin[i].astype(F32)
    weighted = (total * jnp.concatenate([wtv[...], wtv[...]], 1)).astype(BF16)

    def expand(c):
        for b in blocks_of(c):
            part[1, b] = lax.dot_general(
                weighted, wv[b], (((1,), (1,)), ((), ())), preferred_element_type=F32
            ).astype(BF16)

    def prolong(c):
        for b in blocks_of(c):
            l = whole[b].astype(F32)
            rows = jnp.concatenate([l * sign, pltpu.roll(l, BASIS, 1)], 0).astype(BF16)
            both = jnp.dot(rows, basis[b], preferred_element_type=F32)
            out[0, b] = both[:COLS]
            out[1, b] = both[COLS:]

    for c in range(CHUNKS):
        expand(c)
        to_partner(1, c)
    for c in range(CHUNKS):
        along_y(1, c)
    for c in range(CHUNKS + 2):
        if c < CHUNKS:
            whole[mine(c)] = over_y(1, c)
            done = whole.at[mine(c)]
            send(done, done, g_send, g_recv.at[c], partner)
        if c >= 2:
            arrived(whole.at[pl.ds(CHUNK * (c - 2), HALF)], g_recv.at[c - 2])
            prolong(c - 2)
    arrived(ev_in, e_send)
    arrived(core_in, c_send)
    arrived(chip_in, y_send)
    arrived(spec_in, x_send)
    arrived(zin, z_send)
    arrived(whole.at[pl.ds(0, BLOCKS // 2)], g_send)


def write(ready, out, sem):
    copies = []
    for c in range(CHUNKS):
        span = pl.ds(CHUNK * c, CHUNK)
        copies.append(pltpu.make_async_copy(ready.at[:, span], out.at[:, span], sem.at[c]))
        copies[-1].start()
    for copy in copies:
        copy.wait()


def shards(residual, basis, eigvecs, weights):
    hbm_spec = pl.BlockSpec(memory_space=pltpu.HBM)
    vmem_spec = pl.BlockSpec(memory_space=pltpu.VMEM)
    sem = pltpu.SemaphoreType.DMA
    block = (COLS, 2 * BASIS)
    spectral = (COLS, 2 * EIGV)
    args = [
        pltpu.with_memory_space_constraint(a, pltpu.HBM)
        for a in (residual, basis, eigvecs, weights.reshape(1, EIGV))
    ]
    ready = pl.pallas_call(
        coefficients,
        out_shape=jax.ShapeDtypeStruct((2, BLOCKS, COLS, COMP), F32),
        in_specs=[hbm_spec] * 4,
        out_specs=vmem_spec,
        scratch_shapes=[
            pltpu.VMEM((2, BLOCKS, COLS + BASIS, COMP), F32),
            pltpu.VMEM((BLOCKS, 2 * BASIS, COMP), BF16),
            pltpu.VMEM((2, BLOCKS, BASIS, EIGV), BF16),
            pltpu.VMEM((2, CHUNKS, HALF, BASIS, EIGV), BF16),
            pltpu.VMEM((1, EIGV), F32),
            pltpu.VMEM((BLOCKS, 2 * BASIS, 2 * EIGV), BF16),
            pltpu.VMEM((CHUNKS, HALF, 2 * BASIS, 2 * EIGV), BF16),
            pltpu.VMEM((2, BLOCKS, *block), BF16),
            pltpu.VMEM((2, CHUNKS, HALF, *block), BF16),
            pltpu.VMEM((2, CHUNKS, HALF, *block), BF16),
            pltpu.VMEM((2, CHUNKS, Y - 1, HALF, *block), BF16),
            pltpu.VMEM((BLOCKS, *block), BF16),
            pltpu.VMEM((2, *spectral), BF16),
            pltpu.VMEM((2 * X - 1, *spectral), BF16),
            pltpu.VMEM(spectral, BF16),
            pltpu.VMEM((Z - 1, *spectral), BF16),
            sem((BLOCKS // GROUP,)),
            sem((2,)),
            sem,
            sem,
            sem,
            sem((2, CHUNKS)),
            sem,
            sem((2, CHUNKS)),
            sem,
            sem((CHUNKS,)),
            sem,
            sem,
            sem,
            sem,
            pltpu.SemaphoreType.REGULAR,
        ],
        compiler_params=pltpu.CompilerParams(
            collective_id=0, has_side_effects=True, vmem_limit_bytes=24 << 20
        ),
    )(*args)

    return pl.pallas_call(
        write,
        out_shape=jax.ShapeDtypeStruct((2, BLOCKS, COLS, COMP), F32),
        in_specs=[vmem_spec],
        out_specs=hbm_spec,
        scratch_shapes=[sem((CHUNKS,))],
        compiler_params=pltpu.CompilerParams(vmem_limit_bytes=16 << 20),
    )(ready)


def solution(mesh):
    in_specs = (
        P(None, "region", None, "eig"),
        P(None, "region", None, "eig"),
        P(None, "region", None, "eig"),
        P("eig"),
    )
    out_specs = P(None, "region", None, "eig")
    return jax.shard_map(shards, mesh=mesh, in_specs=in_specs, out_specs=out_specs, check_vma=False)
```

```python
import functools

import jax
import jax.numpy as jnp
from jax import lax
from jax.experimental import pallas as pl
from jax.experimental.pallas import tpu as pltpu
from jax.sharding import PartitionSpec as P

MESH = pl.DeviceIdType.MESH
BF16 = jnp.bfloat16
F32 = jnp.float32

BLOCKS = 24
COLS = 32
BASIS = 64
COMP = 384
EIGV = 128
X, Y, Z = 4, 4, 8
CHUNK = 4
HALF = CHUNK // 2
CHUNKS = BLOCKS // CHUNK
BEFORE = 3
GROUP = 4
ALONG_X = (2, 1, 3)
ALONG_Y = (2, 1, 3)
ALONG_Z = (4, 3, 5, 2, 6, 1, 7)
ALONG_Y_CORE = ((2, 0), (2, 1), (1, 0), (1, 1), (3, 0), (3, 1))
ALONG_X_CORE = ((2, 0), (2, 1), (1, 0), (1, 1), (3, 0), (3, 1), (0, 1))


def signs(rows):
    lane = lax.broadcasted_iota(jnp.int32, (rows, 2 * BASIS), 1)
    return jnp.where(lane < BASIS, 1.0, -1.0).astype(F32)


def coefficients(
    res,
    bas,
    eig,
    wts,
    out,
    loaded,
    basis,
    ev,
    ev_in,
    wtv,
    wv,
    wv_in,
    part,
    core_in,
    chip,
    chip_in,
    first_in,
    last_in,
    whole,
    spec,
    spec_in,
    zown,
    zin,
    load_sem,
    eig_sem,
    e_send,
    e_recv,
    c_send,
    c_recv,
    y_send,
    y_recv,
    f_send,
    f_recv,
    l_send,
    l_recv,
    g_send,
    g_recv,
    x_send,
    x_recv,
    z_send,
    z_recv,
    met,
):
    region = lax.axis_index("region")
    me = lax.axis_index("eig")
    x, z = lax.rem(region, X), lax.div(region, X)
    core, y = lax.rem(me, 2), lax.div(me, 2)

    partner = (region, y * 2 + 1 - core)
    x_peers = [
        (z * X + lax.rem(x + d, X), y * 2 + lax.rem(core + dc, 2)) for d, dc in ALONG_X_CORE
    ]
    y_both = [
        (region, lax.rem(y + d, Y) * 2 + lax.rem(core + dc, 2)) for d, dc in ALONG_Y_CORE
    ]
    y_peers = [(region, lax.rem(y + d, Y) * 2 + core) for d in ALONG_Y]
    z_peers = [(lax.rem(z + d, Z) * X + x, me) for d in ALONG_Z]
    barrier = pltpu.get_barrier_semaphore()

    def greet(sem, peer):
        pl.semaphore_signal(sem, inc=1, device_id=peer, device_id_type=MESH)

    for d in ALONG_Z:
        greet(barrier, (lax.rem(z + d, Z) * X + x, y * 2 + 1))
    for d in ALONG_X:
        greet(barrier, (z * X + lax.rem(x + d, X), y * 2 + 1))
    for d in ALONG_Y:
        greet(barrier, (region, lax.rem(y + d, Y) * 2))
    greet(barrier, partner)

    loads = []
    for g in range(BLOCKS // GROUP):
        span = pl.ds(g * GROUP, GROUP)
        into = loaded.at[:, span]
        pltpu.make_async_copy(bas.at[:, span], into.at[:, :, COLS:], load_sem.at[g]).start()
        pltpu.make_async_copy(res.at[:, span], into.at[:, :, :COLS], load_sem.at[g]).start()
        loads.append(into)
    eig_load = pltpu.make_async_copy(eig, ev, eig_sem.at[0])
    wts_load = pltpu.make_async_copy(wts, wtv, eig_sem.at[1])
    eig_load.start()
    wts_load.start()

    def meet_chips(counter, others):
        @pl.when(core == counter)
        def _():
            pl.semaphore_wait(barrier, others)
            greet(met, partner)

        @pl.when(core != counter)
        def _():
            pl.semaphore_wait(met, 1)

    def arrived(ref, sem):
        pltpu.make_async_copy(ref, ref, sem).wait()

    def send(src, dst, send_sem, recv_sem, peer):
        pltpu.make_async_remote_copy(
            src_ref=src,
            dst_ref=dst,
            send_sem=send_sem,
            recv_sem=recv_sem,
            device_id=peer,
            device_id_type=MESH,
        ).start()

    def mine(c):
        return pl.ds(CHUNK * c + HALF * core, HALF)

    def to_partner(w, c):
        theirs = pl.ds(CHUNK * c + HALF * (1 - core), HALF)
        send(part.at[w, theirs], core_in.at[w, c], c_send, c_recv.at[w, c], partner)

    def straight(w):
        to_partner(w, 0)
        for i, ((_, dc), peer) in enumerate(zip(ALONG_Y_CORE, y_both)):
            half = pl.ds(HALF * lax.rem(core + dc, 2), HALF)
            send(part.at[w, half], first_in.at[w, i], f_send, f_recv.at[w], peer)

    def slot(w, c):
        return w * (CHUNKS - 1) + c - 1

    def along_y(w, c):
        arrived(core_in.at[w, c], c_recv.at[w, c])
        total = part[w, mine(c)].astype(F32) + core_in[w, c].astype(F32)
        chip[w, c] = total.astype(BF16)
        if w == 1 and c == CHUNKS - 1:
            for i, peer in enumerate(y_both + [partner]):
                send(chip.at[w, c], last_in.at[i], l_send, l_recv, peer)
        else:
            k = slot(w, c)
            for i, peer in enumerate(y_peers):
                send(chip.at[w, c], chip_in.at[k, i], y_send, y_recv.at[k], peer)

    def over_y(w, c):
        if c == 0:
            arrived(core_in.at[w, c], c_recv.at[w, c])
            arrived(first_in.at[w], f_recv.at[w])
            total = part[w, mine(c)].astype(F32) + core_in[w, c].astype(F32)
            for i in range(len(y_both)):
                total += first_in[w, i].astype(F32)
        else:
            k = slot(w, c)
            arrived(chip_in.at[k], y_recv.at[k])
            total = chip[w, c].astype(F32)
            for i in range(len(y_peers)):
                total += chip_in[k, i].astype(F32)
        return total.astype(BF16)

    def blocks_of(c):
        return range(CHUNK * c, CHUNK * (c + 1))

    sign = signs(COLS)

    def project(c):
        for g in range(c * CHUNK // GROUP, (c + 1) * CHUNK // GROUP):
            arrived(loads[g], load_sem.at[g])
            for b in range(g * GROUP, (g + 1) * GROUP):
                r = jnp.concatenate([loaded[0, b, :COLS], loaded[1, b, :COLS]], 0).astype(BF16)
                k = jnp.concatenate([loaded[0, b, COLS:], loaded[1, b, COLS:]], 0).astype(BF16)
                basis[b] = k
                p = lax.dot_general(r, k, (((1,), (1,)), ((), ())), preferred_element_type=F32)
                part[0, b] = (p[:COLS] * sign + pltpu.roll(p[COLS:], BASIS, 1)).astype(BF16)

    def as_real(to, re, im):
        to[:BASIS, :EIGV] = re
        to[:BASIS, EIGV:] = -im
        to[BASIS:, :EIGV] = im
        to[BASIS:, EIGV:] = re

    def swap():
        eig_load.wait()
        for c in range(CHUNKS):
            theirs = pl.ds(CHUNK * c + HALF * (1 - core), HALF)
            send(ev.at[:, theirs], ev_in.at[:, c], e_send, e_recv, partner)

    for c in range(BEFORE):
        project(c)
    meet_chips(0, 2 * (Y - 1) + 1)
    straight(0)
    for c in range(1, BEFORE):
        to_partner(0, c)
    for c in range(BEFORE, CHUNKS):
        project(c)
        to_partner(0, c)
        if c > BEFORE:
            along_y(0, c - BEFORE)
    for c in range(CHUNKS - BEFORE, CHUNKS):
        along_y(0, c)
    swap()
    for b in range(BLOCKS):
        as_real(wv.at[b], ev[0, b], ev[1, b])
    arrived(ev_in, e_recv)
    for c in range(CHUNKS):
        for i in range(HALF):
            as_real(wv_in.at[c, i], ev_in[0, c, i], ev_in[1, c, i])
    wts_load.wait()
    meet_chips(1, 2 * (X - 1) + 2 * (Z - 1) + 1)
    total = jnp.zeros((COLS, 2 * EIGV), F32)
    other = jnp.zeros((COLS, 2 * EIGV), F32)
    for c in range(CHUNKS):
        half = over_y(0, c)
        for i in range(HALF):
            total += jnp.dot(
                half[i], wv[CHUNK * c + HALF * core + i], preferred_element_type=F32
            )
            other += jnp.dot(half[i], wv_in[c, i], preferred_element_type=F32)

    spec[0] = total.astype(BF16)
    spec[1] = other.astype(BF16)
    for i, (d, peer) in enumerate(zip(ALONG_X_CORE, x_peers)):
        send(spec.at[d[1]], spec_in.at[i], x_send, x_recv, peer)
    arrived(spec_in, x_recv)
    for i in range(len(x_peers)):
        total += spec_in[i].astype(F32)
    zown[...] = total.astype(BF16)
    for i, peer in enumerate(z_peers):
        send(zown, zin.at[i], z_send, z_recv, peer)
    arrived(zin, z_recv)
    for i in range(len(z_peers)):
        total += zin[i].astype(F32)
    weighted = (total * jnp.concatenate([wtv[...], wtv[...]], 1)).astype(BF16)

    def expand(c):
        for b in blocks_of(c):
            part[1, b] = lax.dot_general(
                weighted, wv[b], (((1,), (1,)), ((), ())), preferred_element_type=F32
            ).astype(BF16)

    def prolong(c):
        for b in blocks_of(c):
            l = whole[b].astype(F32)
            rows = jnp.concatenate([l * sign, pltpu.roll(l, BASIS, 1)], 0).astype(BF16)
            both = jnp.dot(rows, basis[b], preferred_element_type=F32)
            out[0, b] = both[:COLS]
            out[1, b] = both[COLS:]

    expand(0)
    straight(1)
    for c in range(1, CHUNKS):
        expand(c)
        to_partner(1, c)
    for c in range(1, CHUNKS):
        along_y(1, c)
    last = CHUNKS - 1
    for c in range(last + 2):
        if c < last:
            whole[mine(c)] = over_y(1, c)
            done = whole.at[mine(c)]
            send(done, done, g_send, g_recv.at[c], partner)
        if c >= 2:
            arrived(whole.at[pl.ds(CHUNK * (c - 2), HALF)], g_recv.at[c - 2])
            prolong(c - 2)
    arrived(last_in, l_recv)
    ours = chip[1, last].astype(F32)
    theirs = last_in[len(y_both)].astype(F32)
    for i, (_, dc) in enumerate(ALONG_Y_CORE):
        if dc == 0:
            ours += last_in[i].astype(F32)
        else:
            theirs += last_in[i].astype(F32)
    whole[mine(last)] = ours.astype(BF16)
    whole[pl.ds(CHUNK * last + HALF * (1 - core), HALF)] = theirs.astype(BF16)
    prolong(last)
    arrived(ev_in, e_send)
    arrived(core_in, c_send)
    arrived(chip_in, y_send)
    arrived(first_in, f_send)
    arrived(last_in, l_send)
    arrived(spec_in, x_send)
    arrived(zin, z_send)
    arrived(whole.at[pl.ds(0, HALF * (CHUNKS - 1))], g_send)


def write(ready, out, sem):
    copies = []
    for c in range(CHUNKS):
        span = pl.ds(CHUNK * c, CHUNK)
        copies.append(pltpu.make_async_copy(ready.at[:, span], out.at[:, span], sem.at[c]))
        copies[-1].start()
    for copy in copies:
        copy.wait()


def shards(residual, basis, eigvecs, weights):
    hbm_spec = pl.BlockSpec(memory_space=pltpu.HBM)
    vmem_spec = pl.BlockSpec(memory_space=pltpu.VMEM)
    sem = pltpu.SemaphoreType.DMA
    block = (COLS, 2 * BASIS)
    spectral = (COLS, 2 * EIGV)
    args = [
        pltpu.with_memory_space_constraint(a, pltpu.HBM)
        for a in (residual, basis, eigvecs, weights.reshape(1, EIGV))
    ]
    ready = pl.pallas_call(
        coefficients,
        out_shape=jax.ShapeDtypeStruct((2, BLOCKS, COLS, COMP), F32),
        in_specs=[hbm_spec] * 4,
        out_specs=vmem_spec,
        scratch_shapes=[
            pltpu.VMEM((2, BLOCKS, COLS + BASIS, COMP), F32),
            pltpu.VMEM((BLOCKS, 2 * BASIS, COMP), BF16),
            pltpu.VMEM((2, BLOCKS, BASIS, EIGV), BF16),
            pltpu.VMEM((2, CHUNKS, HALF, BASIS, EIGV), BF16),
            pltpu.VMEM((1, EIGV), F32),
            pltpu.VMEM((BLOCKS, 2 * BASIS, 2 * EIGV), BF16),
            pltpu.VMEM((CHUNKS, HALF, 2 * BASIS, 2 * EIGV), BF16),
            pltpu.VMEM((2, BLOCKS, *block), BF16),
            pltpu.VMEM((2, CHUNKS, HALF, *block), BF16),
            pltpu.VMEM((2, CHUNKS, HALF, *block), BF16),
            pltpu.VMEM((2 * CHUNKS - 3, Y - 1, HALF, *block), BF16),
            pltpu.VMEM((2, 2 * Y - 2, HALF, *block), BF16),
            pltpu.VMEM((2 * Y - 1, HALF, *block), BF16),
            pltpu.VMEM((BLOCKS, *block), BF16),
            pltpu.VMEM((2, *spectral), BF16),
            pltpu.VMEM((2 * X - 1, *spectral), BF16),
            pltpu.VMEM(spectral, BF16),
            pltpu.VMEM((Z - 1, *spectral), BF16),
            sem((BLOCKS // GROUP,)),
            sem((2,)),
            sem,
            sem,
            sem,
            sem((2, CHUNKS)),
            sem,
            sem((2 * CHUNKS - 3,)),
            sem,
            sem((2,)),
            sem,
            sem,
            sem,
            sem((CHUNKS - 1,)),
            sem,
            sem,
            sem,
            sem,
            pltpu.SemaphoreType.REGULAR,
        ],
        compiler_params=pltpu.CompilerParams(
            collective_id=0, has_side_effects=True, vmem_limit_bytes=24 << 20
        ),
    )(*args)

    return pl.pallas_call(
        write,
        out_shape=jax.ShapeDtypeStruct((2, BLOCKS, COLS, COMP), F32),
        in_specs=[vmem_spec],
        out_specs=hbm_spec,
        scratch_shapes=[sem((CHUNKS,))],
        compiler_params=pltpu.CompilerParams(vmem_limit_bytes=16 << 20),
    )(ready)


def solution(mesh):
    in_specs = (
        P(None, "region", None, "eig"),
        P(None, "region", None, "eig"),
        P(None, "region", None, "eig"),
        P("eig"),
    )
    out_specs = P(None, "region", None, "eig")
    return jax.shard_map(shards, mesh=mesh, in_specs=in_specs, out_specs=out_specs, check_vma=False)
```

```python
import functools

import jax
import jax.numpy as jnp
from jax import lax
from jax.experimental import pallas as pl
from jax.experimental.pallas import tpu as pltpu
from jax.sharding import PartitionSpec as P

MESH = pl.DeviceIdType.MESH
BF16 = jnp.bfloat16
F32 = jnp.float32

BLOCKS = 24
COLS = 32
BASIS = 64
COMP = 384
EIGV = 128
X, Y, Z = 4, 4, 8
CHUNK = 4
HALF = CHUNK // 2
CHUNKS = BLOCKS // CHUNK
EARLY = 4
BEFORE = 3
GROUP = 4
ALONG_X = (2, 1, 3)
ALONG_Y = (2, 1, 3)
ALONG_Z = (4, 3, 5, 2, 6, 1, 7)
ALONG_Y_CORE = ((2, 0), (2, 1), (1, 0), (1, 1), (3, 0), (3, 1))
ALONG_X_CORE = ((2, 0), (2, 1), (1, 0), (1, 1), (3, 0), (3, 1), (0, 1))


def signs(rows):
    lane = lax.broadcasted_iota(jnp.int32, (rows, 2 * BASIS), 1)
    return jnp.where(lane < BASIS, 1.0, -1.0).astype(F32)


def prolong(lift, bas, sign):
    l = lift.astype(F32)
    rows = jnp.concatenate([l * sign, pltpu.roll(l, BASIS, 1)], 0).astype(BF16)
    return jnp.dot(rows, bas, preferred_element_type=F32)


def coefficients(
    res,
    bas,
    eig,
    wts,
    out,
    lift_out,
    basis,
    loaded,
    ev,
    ev_in,
    wtv,
    wv,
    wv_in,
    part,
    core_in,
    chip,
    chip_in,
    first_in,
    last_in,
    whole,
    spec,
    spec_in,
    zown,
    zin,
    load_sem,
    eig_sem,
    e_send,
    e_recv,
    c_send,
    c_recv,
    y_send,
    y_recv,
    f_send,
    f_recv,
    l_send,
    l_recv,
    g_send,
    g_recv,
    x_send,
    x_recv,
    z_send,
    z_recv,
    met,
):
    region = lax.axis_index("region")
    me = lax.axis_index("eig")
    x, z = lax.rem(region, X), lax.div(region, X)
    core, y = lax.rem(me, 2), lax.div(me, 2)

    partner = (region, y * 2 + 1 - core)
    x_peers = [
        (z * X + lax.rem(x + d, X), y * 2 + lax.rem(core + dc, 2)) for d, dc in ALONG_X_CORE
    ]
    y_both = [
        (region, lax.rem(y + d, Y) * 2 + lax.rem(core + dc, 2)) for d, dc in ALONG_Y_CORE
    ]
    y_peers = [(region, lax.rem(y + d, Y) * 2 + core) for d in ALONG_Y]
    z_peers = [(lax.rem(z + d, Z) * X + x, me) for d in ALONG_Z]
    barrier = pltpu.get_barrier_semaphore()

    def greet(sem, peer):
        pl.semaphore_signal(sem, inc=1, device_id=peer, device_id_type=MESH)

    for d in ALONG_Y:
        greet(barrier, (region, lax.rem(y + d, Y) * 2))
    greet(barrier, partner)

    loads = []
    for g in range(BLOCKS // GROUP):
        span = pl.ds(g * GROUP, GROUP)
        into = loaded.at[:, span]
        pltpu.make_async_copy(bas.at[:, span], into.at[:, :, COLS:], load_sem.at[g]).start()
        pltpu.make_async_copy(res.at[:, span], into.at[:, :, :COLS], load_sem.at[g]).start()
        loads.append(into)
    eig_load = pltpu.make_async_copy(eig, ev, eig_sem.at[0])
    wts_load = pltpu.make_async_copy(wts, wtv, eig_sem.at[1])
    eig_load.start()
    wts_load.start()

    for d in ALONG_Z:
        greet(barrier, (lax.rem(z + d, Z) * X + x, y * 2 + 1))
    for d in ALONG_X:
        greet(barrier, (z * X + lax.rem(x + d, X), y * 2 + 1))
    def meet_chips(counter, others):
        @pl.when(core == counter)
        def _():
            pl.semaphore_wait(barrier, others)
            greet(met, partner)

        @pl.when(core != counter)
        def _():
            pl.semaphore_wait(met, 1)

    def arrived(ref, sem):
        pltpu.make_async_copy(ref, ref, sem).wait()

    def send(src, dst, send_sem, recv_sem, peer):
        pltpu.make_async_remote_copy(
            src_ref=src,
            dst_ref=dst,
            send_sem=send_sem,
            recv_sem=recv_sem,
            device_id=peer,
            device_id_type=MESH,
        ).start()

    def mine(c):
        return pl.ds(CHUNK * c + HALF * core, HALF)

    def to_partner(w, c):
        theirs = pl.ds(CHUNK * c + HALF * (1 - core), HALF)
        send(part.at[w, theirs], core_in.at[w, c], c_send, c_recv.at[w, c], partner)

    def straight(w):
        to_partner(w, 0)
        for i, ((_, dc), peer) in enumerate(zip(ALONG_Y_CORE, y_both)):
            half = pl.ds(HALF * lax.rem(core + dc, 2), HALF)
            send(part.at[w, half], first_in.at[w, i], f_send, f_recv.at[w], peer)

    def slot(w, c):
        return w * (CHUNKS - 1) + c - 1

    def along_y(w, c):
        arrived(core_in.at[w, c], c_recv.at[w, c])
        total = part[w, mine(c)].astype(F32) + core_in[w, c].astype(F32)
        chip[w, c] = total.astype(BF16)
        if w == 1 and c == CHUNKS - 1:
            for i, peer in enumerate(y_both + [partner]):
                send(chip.at[w, c], last_in.at[i], l_send, l_recv, peer)
        else:
            k = slot(w, c)
            for i, peer in enumerate(y_peers):
                send(chip.at[w, c], chip_in.at[k, i], y_send, y_recv.at[k], peer)

    def over_y(w, c):
        if c == 0:
            arrived(core_in.at[w, c], c_recv.at[w, c])
            arrived(first_in.at[w], f_recv.at[w])
            total = part[w, mine(c)].astype(F32) + core_in[w, c].astype(F32)
            for i in range(len(y_both)):
                total += first_in[w, i].astype(F32)
        else:
            k = slot(w, c)
            arrived(chip_in.at[k], y_recv.at[k])
            total = chip[w, c].astype(F32)
            for i in range(len(y_peers)):
                total += chip_in[k, i].astype(F32)
        return total.astype(BF16)

    def blocks_of(c):
        return range(CHUNK * c, CHUNK * (c + 1))

    sign = signs(COLS)

    def project(c):
        for g in range(c * CHUNK // GROUP, (c + 1) * CHUNK // GROUP):
            arrived(loads[g], load_sem.at[g])
            for b in range(g * GROUP, (g + 1) * GROUP):
                r = jnp.concatenate([loaded[0, b, :COLS], loaded[1, b, :COLS]], 0).astype(BF16)
                k = jnp.concatenate([loaded[0, b, COLS:], loaded[1, b, COLS:]], 0).astype(BF16)
                basis[b] = k
                p = lax.dot_general(r, k, (((1,), (1,)), ((), ())), preferred_element_type=F32)
                part[0, b] = (p[:COLS] * sign + pltpu.roll(p[COLS:], BASIS, 1)).astype(BF16)

    def as_real(to, re, im):
        to[:BASIS, :EIGV] = re
        to[:BASIS, EIGV:] = -im
        to[BASIS:, :EIGV] = im
        to[BASIS:, EIGV:] = re

    def swap():
        eig_load.wait()
        for c in range(CHUNKS):
            theirs = pl.ds(CHUNK * c + HALF * (1 - core), HALF)
            send(ev.at[:, theirs], ev_in.at[:, c], e_send, e_recv, partner)

    for c in range(BEFORE):
        project(c)
    meet_chips(0, 2 * (Y - 1) + 1)
    straight(0)
    for c in range(1, BEFORE):
        to_partner(0, c)
    for c in range(BEFORE, CHUNKS):
        project(c)
        to_partner(0, c)
        if c > BEFORE:
            along_y(0, c - BEFORE)
    for c in range(CHUNKS - BEFORE, CHUNKS):
        along_y(0, c)
    swap()
    for b in range(BLOCKS):
        as_real(wv.at[b], ev[0, b], ev[1, b])
    arrived(ev_in, e_recv)
    for c in range(CHUNKS):
        for i in range(HALF):
            as_real(wv_in.at[c, i], ev_in[0, c, i], ev_in[1, c, i])
    wts_load.wait()
    meet_chips(1, 2 * (X - 1) + 2 * (Z - 1) + 1)
    total = jnp.zeros((COLS, 2 * EIGV), F32)
    other = jnp.zeros((COLS, 2 * EIGV), F32)
    for c in range(CHUNKS):
        half = over_y(0, c)
        for i in range(HALF):
            total += jnp.dot(
                half[i], wv[CHUNK * c + HALF * core + i], preferred_element_type=F32
            )
            other += jnp.dot(half[i], wv_in[c, i], preferred_element_type=F32)

    spec[0] = total.astype(BF16)
    spec[1] = other.astype(BF16)
    for i, (d, peer) in enumerate(zip(ALONG_X_CORE, x_peers)):
        send(spec.at[d[1]], spec_in.at[i], x_send, x_recv, peer)
    arrived(spec_in, x_recv)
    for i in range(len(x_peers)):
        total += spec_in[i].astype(F32)
    zown[...] = total.astype(BF16)
    for i, peer in enumerate(z_peers):
        send(zown, zin.at[i], z_send, z_recv, peer)
    arrived(zin, z_recv)
    for i in range(len(z_peers)):
        total += zin[i].astype(F32)
    weighted = (total * jnp.concatenate([wtv[...], wtv[...]], 1)).astype(BF16)

    def expand(c):
        for b in blocks_of(c):
            part[1, b] = lax.dot_general(
                weighted, wv[b], (((1,), (1,)), ((), ())), preferred_element_type=F32
            ).astype(BF16)

    expand(0)
    straight(1)
    for c in range(1, CHUNKS):
        expand(c)
        to_partner(1, c)
    for c in range(1, CHUNKS):
        along_y(1, c)
    last = CHUNKS - 1
    for c in range(last + 2):
        if c < last:
            whole[mine(c)] = over_y(1, c)
            done = whole.at[mine(c)]
            send(done, done, g_send, g_recv.at[c], partner)
        if c >= 2:
            arrived(whole.at[pl.ds(CHUNK * (c - 2), HALF)], g_recv.at[c - 2])
            for b in blocks_of(c - 2):
                if c - 2 < EARLY:
                    both = prolong(whole[b], basis[b], sign)
                    out[0, b] = both[:COLS]
                    out[1, b] = both[COLS:]
                else:
                    lift_out[b - CHUNK * EARLY] = whole[b]
    arrived(last_in, l_recv)
    ours = chip[1, last].astype(F32)
    theirs = last_in[len(y_both)].astype(F32)
    for i, (_, dc) in enumerate(ALONG_Y_CORE):
        if dc == 0:
            ours += last_in[i].astype(F32)
        else:
            theirs += last_in[i].astype(F32)
    first = CHUNK * (last - EARLY)
    lift_out[pl.ds(first + HALF * core, HALF)] = ours.astype(BF16)
    lift_out[pl.ds(first + HALF * (1 - core), HALF)] = theirs.astype(BF16)
    arrived(ev_in, e_send)
    arrived(core_in, c_send)
    arrived(chip_in, y_send)
    arrived(first_in, f_send)
    arrived(last_in, l_send)
    arrived(spec_in, x_send)
    arrived(zin, z_send)
    arrived(whole.at[pl.ds(0, HALF * (CHUNKS - 1))], g_send)


def write(ready, lift, basis, out, rest, sem):
    sign = signs(COLS)
    copies = []

    def start(c, source):
        span = pl.ds(CHUNK * c, CHUNK)
        copies.append(pltpu.make_async_copy(source, out.at[:, span], sem.at[c]))
        copies[-1].start()

    for c in range(EARLY):
        start(c, ready.at[:, pl.ds(CHUNK * c, CHUNK)])
    for c in range(EARLY, CHUNKS):
        for b in range(CHUNK * (c - EARLY), CHUNK * (c - EARLY + 1)):
            both = prolong(lift[b], basis[CHUNK * EARLY + b], sign)
            rest[0, b] = both[:COLS]
            rest[1, b] = both[COLS:]
        start(c, rest.at[:, pl.ds(CHUNK * (c - EARLY), CHUNK)])
    for copy in copies:
        copy.wait()


def shards(residual, basis, eigvecs, weights):
    hbm_spec = pl.BlockSpec(memory_space=pltpu.HBM)
    vmem_spec = pl.BlockSpec(memory_space=pltpu.VMEM)
    sem = pltpu.SemaphoreType.DMA
    block = (COLS, 2 * BASIS)
    spectral = (COLS, 2 * EIGV)
    args = [
        pltpu.with_memory_space_constraint(a, pltpu.HBM)
        for a in (residual, basis, eigvecs, weights.reshape(1, EIGV))
    ]
    early = CHUNK * EARLY
    done = pl.pallas_call(
        coefficients,
        out_shape=(
            jax.ShapeDtypeStruct((2, early, COLS, COMP), F32),
            jax.ShapeDtypeStruct((BLOCKS - early, *block), BF16),
            jax.ShapeDtypeStruct((BLOCKS, 2 * BASIS, COMP), BF16),
        ),
        in_specs=[hbm_spec] * 4,
        out_specs=(vmem_spec, vmem_spec, vmem_spec),
        scratch_shapes=[
            pltpu.VMEM((2, BLOCKS, COLS + BASIS, COMP), F32),
            pltpu.VMEM((2, BLOCKS, BASIS, EIGV), BF16),
            pltpu.VMEM((2, CHUNKS, HALF, BASIS, EIGV), BF16),
            pltpu.VMEM((1, EIGV), F32),
            pltpu.VMEM((BLOCKS, 2 * BASIS, 2 * EIGV), BF16),
            pltpu.VMEM((CHUNKS, HALF, 2 * BASIS, 2 * EIGV), BF16),
            pltpu.VMEM((2, BLOCKS, *block), BF16),
            pltpu.VMEM((2, CHUNKS, HALF, *block), BF16),
            pltpu.VMEM((2, CHUNKS, HALF, *block), BF16),
            pltpu.VMEM((2 * CHUNKS - 3, Y - 1, HALF, *block), BF16),
            pltpu.VMEM((2, 2 * Y - 2, HALF, *block), BF16),
            pltpu.VMEM((2 * Y - 1, HALF, *block), BF16),
            pltpu.VMEM((BLOCKS, *block), BF16),
            pltpu.VMEM((2, *spectral), BF16),
            pltpu.VMEM((2 * X - 1, *spectral), BF16),
            pltpu.VMEM(spectral, BF16),
            pltpu.VMEM((Z - 1, *spectral), BF16),
            sem((BLOCKS // GROUP,)),
            sem((2,)),
            sem,
            sem,
            sem,
            sem((2, CHUNKS)),
            sem,
            sem((2 * CHUNKS - 3,)),
            sem,
            sem((2,)),
            sem,
            sem,
            sem,
            sem((CHUNKS - 1,)),
            sem,
            sem,
            sem,
            sem,
            pltpu.SemaphoreType.REGULAR,
        ],
        compiler_params=pltpu.CompilerParams(
            collective_id=0, has_side_effects=True, vmem_limit_bytes=24 << 20
        ),
    )(*args)

    return pl.pallas_call(
        write,
        out_shape=jax.ShapeDtypeStruct((2, BLOCKS, COLS, COMP), F32),
        in_specs=[vmem_spec] * 3,
        out_specs=hbm_spec,
        scratch_shapes=[
            pltpu.VMEM((2, BLOCKS - early, COLS, COMP), F32),
            sem((CHUNKS,)),
        ],
        compiler_params=pltpu.CompilerParams(vmem_limit_bytes=16 << 20),
    )(*done)


def solution(mesh):
    in_specs = (
        P(None, "region", None, "eig"),
        P(None, "region", None, "eig"),
        P(None, "region", None, "eig"),
        P("eig"),
    )
    out_specs = P(None, "region", None, "eig")
    return jax.shard_map(shards, mesh=mesh, in_specs=in_specs, out_specs=out_specs, check_vma=False)
```

```python
import functools

import jax
import jax.numpy as jnp
from jax import lax
from jax.experimental import pallas as pl
from jax.experimental.pallas import tpu as pltpu
from jax.sharding import PartitionSpec as P

MESH = pl.DeviceIdType.MESH
BF16 = jnp.bfloat16
F32 = jnp.float32

BLOCKS = 24
COLS = 32
BASIS = 64
COMP = 384
EIGV = 128
X, Y, Z = 4, 4, 8
CHUNK = 4
HALF = CHUNK // 2
CHUNKS = BLOCKS // CHUNK
EARLY = 4
JOINED = (3, 2)
BEFORE = 3
GROUP = 4
ALONG_X = (2, 1, 3)
ALONG_Y = (2, 1, 3)
ALONG_Z = (4, 3, 5, 2, 6, 1, 7)
ALONG_Y_CORE = ((2, 0), (2, 1), (1, 0), (1, 1), (3, 0), (3, 1))
ALONG_X_CORE = ((2, 0), (2, 1), (1, 0), (1, 1), (3, 0), (3, 1), (0, 1))


def signs(rows):
    lane = lax.broadcasted_iota(jnp.int32, (rows, 2 * BASIS), 1)
    return jnp.where(lane < BASIS, 1.0, -1.0).astype(F32)


def prolong(lift, bas, sign):
    l = lift.astype(F32)
    rows = jnp.concatenate([l * sign, pltpu.roll(l, BASIS, 1)], 0).astype(BF16)
    return jnp.dot(rows, bas, preferred_element_type=F32)


def coefficients(
    res,
    bas,
    eig,
    wts,
    out,
    lift_out,
    basis,
    loaded,
    ev,
    ev_in,
    wtv,
    wv,
    wv_in,
    part,
    core_in,
    chip,
    chip_in,
    first_in,
    last_in,
    whole,
    spec,
    spec_in,
    zown,
    zin,
    load_sem,
    eig_sem,
    e_send,
    e_recv,
    c_send,
    c_recv,
    y_send,
    y_recv,
    f_send,
    f_recv,
    l_send,
    l_recv,
    g_send,
    g_recv,
    x_send,
    x_recv,
    z_send,
    z_recv,
    met,
):
    region = lax.axis_index("region")
    me = lax.axis_index("eig")
    x, z = lax.rem(region, X), lax.div(region, X)
    core, y = lax.rem(me, 2), lax.div(me, 2)

    partner = (region, y * 2 + 1 - core)
    x_peers = [
        (z * X + lax.rem(x + d, X), y * 2 + lax.rem(core + dc, 2)) for d, dc in ALONG_X_CORE
    ]
    y_both = [
        (region, lax.rem(y + d, Y) * 2 + lax.rem(core + dc, 2)) for d, dc in ALONG_Y_CORE
    ]
    y_peers = [(region, lax.rem(y + d, Y) * 2 + core) for d in ALONG_Y]
    z_peers = [(lax.rem(z + d, Z) * X + x, me) for d in ALONG_Z]
    barrier = pltpu.get_barrier_semaphore()

    def greet(sem, peer):
        pl.semaphore_signal(sem, inc=1, device_id=peer, device_id_type=MESH)

    for d in ALONG_Y:
        greet(barrier, (region, lax.rem(y + d, Y) * 2))
    greet(barrier, partner)

    loads = []
    for g in range(BLOCKS // GROUP):
        span = pl.ds(g * GROUP, GROUP)
        into = loaded.at[:, span]
        pltpu.make_async_copy(bas.at[:, span], into.at[:, :, COLS:], load_sem.at[g]).start()
        pltpu.make_async_copy(res.at[:, span], into.at[:, :, :COLS], load_sem.at[g]).start()
        loads.append(into)
    eig_load = pltpu.make_async_copy(eig, ev, eig_sem.at[0])
    wts_load = pltpu.make_async_copy(wts, wtv, eig_sem.at[1])
    eig_load.start()
    wts_load.start()

    for d in ALONG_Z:
        greet(barrier, (lax.rem(z + d, Z) * X + x, y * 2 + 1))
    for d in ALONG_X:
        greet(barrier, (z * X + lax.rem(x + d, X), y * 2 + 1))
    def meet_chips(counter, others):
        @pl.when(core == counter)
        def _():
            pl.semaphore_wait(barrier, others)
            greet(met, partner)

        @pl.when(core != counter)
        def _():
            pl.semaphore_wait(met, 1)

    def arrived(ref, sem):
        pltpu.make_async_copy(ref, ref, sem).wait()

    def send(src, dst, send_sem, recv_sem, peer):
        pltpu.make_async_remote_copy(
            src_ref=src,
            dst_ref=dst,
            send_sem=send_sem,
            recv_sem=recv_sem,
            device_id=peer,
            device_id_type=MESH,
        ).start()

    def mine(c):
        return pl.ds(CHUNK * c + HALF * core, HALF)

    def to_partner(w, c):
        theirs = pl.ds(CHUNK * c + HALF * (1 - core), HALF)
        send(part.at[w, theirs], core_in.at[w, c], c_send, c_recv.at[w, max(c - JOINED[w] + 1, 0)], partner)

    def straight(w):
        to_partner(w, 0)
        for i, ((_, dc), peer) in enumerate(zip(ALONG_Y_CORE, y_both)):
            half = pl.ds(HALF * lax.rem(core + dc, 2), HALF)
            send(part.at[w, half], first_in.at[w, i], f_send, f_recv.at[w], peer)

    def slot(w, c):
        return w * (CHUNKS - 1) + c - 1

    def along_y(w, c):
        if c == 1:
            arrived(core_in.at[w, pl.ds(0, JOINED[w])], c_recv.at[w, 0])
        elif c >= JOINED[w]:
            arrived(core_in.at[w, c], c_recv.at[w, c - JOINED[w] + 1])
        total = part[w, mine(c)].astype(F32) + core_in[w, c].astype(F32)
        chip[w, c] = total.astype(BF16)
        if w == 1 and c == CHUNKS - 1:
            for i, peer in enumerate(y_both + [partner]):
                send(chip.at[w, c], last_in.at[i], l_send, l_recv, peer)
        else:
            k = slot(w, c)
            for i, peer in enumerate(y_peers):
                send(chip.at[w, c], chip_in.at[k, i], y_send, y_recv.at[k], peer)

    def over_y(w, c):
        if c == 0:
            arrived(first_in.at[w], f_recv.at[w])
            total = part[w, mine(c)].astype(F32) + core_in[w, c].astype(F32)
            for i in range(len(y_both)):
                total += first_in[w, i].astype(F32)
        else:
            k = slot(w, c)
            arrived(chip_in.at[k], y_recv.at[k])
            total = chip[w, c].astype(F32)
            for i in range(len(y_peers)):
                total += chip_in[k, i].astype(F32)
        return total.astype(BF16)

    def blocks_of(c):
        return range(CHUNK * c, CHUNK * (c + 1))

    sign = signs(COLS)

    def project(c):
        for g in range(c * CHUNK // GROUP, (c + 1) * CHUNK // GROUP):
            arrived(loads[g], load_sem.at[g])
            for b in range(g * GROUP, (g + 1) * GROUP):
                r = jnp.concatenate([loaded[0, b, :COLS], loaded[1, b, :COLS]], 0).astype(BF16)
                k = jnp.concatenate([loaded[0, b, COLS:], loaded[1, b, COLS:]], 0).astype(BF16)
                basis[b] = k
                p = lax.dot_general(r, k, (((1,), (1,)), ((), ())), preferred_element_type=F32)
                part[0, b] = (p[:COLS] * sign + pltpu.roll(p[COLS:], BASIS, 1)).astype(BF16)

    def as_real(to, re, im):
        to[:BASIS, :EIGV] = re
        to[:BASIS, EIGV:] = -im
        to[BASIS:, :EIGV] = im
        to[BASIS:, EIGV:] = re

    def swap():
        eig_load.wait()
        for c in range(CHUNKS):
            theirs = pl.ds(CHUNK * c + HALF * (1 - core), HALF)
            send(ev.at[:, theirs], ev_in.at[:, c], e_send, e_recv, partner)

    for c in range(BEFORE):
        project(c)
    meet_chips(0, 2 * (Y - 1) + 1)
    straight(0)
    for c in range(1, BEFORE):
        to_partner(0, c)
    for c in range(BEFORE, CHUNKS):
        project(c)
        to_partner(0, c)
        if c > BEFORE:
            along_y(0, c - BEFORE)
    for c in range(CHUNKS - BEFORE, CHUNKS):
        along_y(0, c)
    swap()
    for b in range(BLOCKS):
        as_real(wv.at[b], ev[0, b], ev[1, b])
    arrived(ev_in, e_recv)
    for c in range(CHUNKS):
        for i in range(HALF):
            as_real(wv_in.at[c, i], ev_in[0, c, i], ev_in[1, c, i])
    wts_load.wait()
    meet_chips(1, 2 * (X - 1) + 2 * (Z - 1) + 1)
    total = jnp.zeros((COLS, 2 * EIGV), F32)
    other = jnp.zeros((COLS, 2 * EIGV), F32)
    for c in range(CHUNKS):
        half = over_y(0, c)
        for i in range(HALF):
            total += jnp.dot(
                half[i], wv[CHUNK * c + HALF * core + i], preferred_element_type=F32
            )
            other += jnp.dot(half[i], wv_in[c, i], preferred_element_type=F32)

    spec[0] = total.astype(BF16)
    spec[1] = other.astype(BF16)
    for i, (d, peer) in enumerate(zip(ALONG_X_CORE, x_peers)):
        send(spec.at[d[1]], spec_in.at[i], x_send, x_recv, peer)
    arrived(spec_in, x_recv)
    for i in range(len(x_peers)):
        total += spec_in[i].astype(F32)
    zown[...] = total.astype(BF16)
    for i, peer in enumerate(z_peers):
        send(zown, zin.at[i], z_send, z_recv, peer)
    arrived(zin, z_recv)
    for i in range(len(z_peers)):
        total += zin[i].astype(F32)
    weighted = (total * jnp.concatenate([wtv[...], wtv[...]], 1)).astype(BF16)

    def expand(c):
        for b in blocks_of(c):
            part[1, b] = lax.dot_general(
                weighted, wv[b], (((1,), (1,)), ((), ())), preferred_element_type=F32
            ).astype(BF16)

    expand(0)
    straight(1)
    for c in range(1, CHUNKS):
        expand(c)
        to_partner(1, c)
    for c in range(1, CHUNKS):
        along_y(1, c)
    last = CHUNKS - 1
    for c in range(last + 2):
        if c < last:
            whole[mine(c)] = over_y(1, c)
            done = whole.at[mine(c)]
            send(done, done, g_send, g_recv.at[c], partner)
        if c >= 2:
            arrived(whole.at[pl.ds(CHUNK * (c - 2), HALF)], g_recv.at[c - 2])
            for b in blocks_of(c - 2):
                if c - 2 < EARLY:
                    both = prolong(whole[b], basis[b], sign)
                    out[0, b] = both[:COLS]
                    out[1, b] = both[COLS:]
                else:
                    lift_out[b - CHUNK * EARLY] = whole[b]
    arrived(last_in, l_recv)
    ours = chip[1, last].astype(F32)
    theirs = last_in[len(y_both)].astype(F32)
    for i, (_, dc) in enumerate(ALONG_Y_CORE):
        if dc == 0:
            ours += last_in[i].astype(F32)
        else:
            theirs += last_in[i].astype(F32)
    first = CHUNK * (last - EARLY)
    lift_out[pl.ds(first + HALF * core, HALF)] = ours.astype(BF16)
    lift_out[pl.ds(first + HALF * (1 - core), HALF)] = theirs.astype(BF16)
    arrived(ev_in, e_send)
    arrived(core_in, c_send)
    arrived(chip_in, y_send)
    arrived(first_in, f_send)
    arrived(last_in, l_send)
    arrived(spec_in, x_send)
    arrived(zin, z_send)
    arrived(whole.at[pl.ds(0, HALF * (CHUNKS - 1))], g_send)


def write(ready, lift, basis, out, rest, sem):
    sign = signs(COLS)
    copies = []

    def start(c, source):
        span = pl.ds(CHUNK * c, CHUNK)
        copies.append(pltpu.make_async_copy(source, out.at[:, span], sem.at[c]))
        copies[-1].start()

    for c in range(EARLY):
        start(c, ready.at[:, pl.ds(CHUNK * c, CHUNK)])
    for c in range(EARLY, CHUNKS):
        for b in range(CHUNK * (c - EARLY), CHUNK * (c - EARLY + 1)):
            both = prolong(lift[b], basis[CHUNK * EARLY + b], sign)
            rest[0, b] = both[:COLS]
            rest[1, b] = both[COLS:]
        start(c, rest.at[:, pl.ds(CHUNK * (c - EARLY), CHUNK)])
    for copy in copies:
        copy.wait()


def shards(residual, basis, eigvecs, weights):
    hbm_spec = pl.BlockSpec(memory_space=pltpu.HBM)
    vmem_spec = pl.BlockSpec(memory_space=pltpu.VMEM)
    sem = pltpu.SemaphoreType.DMA
    block = (COLS, 2 * BASIS)
    spectral = (COLS, 2 * EIGV)
    args = [
        pltpu.with_memory_space_constraint(a, pltpu.HBM)
        for a in (residual, basis, eigvecs, weights.reshape(1, EIGV))
    ]
    early = CHUNK * EARLY
    done = pl.pallas_call(
        coefficients,
        out_shape=(
            jax.ShapeDtypeStruct((2, early, COLS, COMP), F32),
            jax.ShapeDtypeStruct((BLOCKS - early, *block), BF16),
            jax.ShapeDtypeStruct((BLOCKS, 2 * BASIS, COMP), BF16),
        ),
        in_specs=[hbm_spec] * 4,
        out_specs=(vmem_spec, vmem_spec, vmem_spec),
        scratch_shapes=[
            pltpu.VMEM((2, BLOCKS, COLS + BASIS, COMP), F32),
            pltpu.VMEM((2, BLOCKS, BASIS, EIGV), BF16),
            pltpu.VMEM((2, CHUNKS, HALF, BASIS, EIGV), BF16),
            pltpu.VMEM((1, EIGV), F32),
            pltpu.VMEM((BLOCKS, 2 * BASIS, 2 * EIGV), BF16),
            pltpu.VMEM((CHUNKS, HALF, 2 * BASIS, 2 * EIGV), BF16),
            pltpu.VMEM((2, BLOCKS, *block), BF16),
            pltpu.VMEM((2, CHUNKS, HALF, *block), BF16),
            pltpu.VMEM((2, CHUNKS, HALF, *block), BF16),
            pltpu.VMEM((2 * CHUNKS - 3, Y - 1, HALF, *block), BF16),
            pltpu.VMEM((2, 2 * Y - 2, HALF, *block), BF16),
            pltpu.VMEM((2 * Y - 1, HALF, *block), BF16),
            pltpu.VMEM((BLOCKS, *block), BF16),
            pltpu.VMEM((2, *spectral), BF16),
            pltpu.VMEM((2 * X - 1, *spectral), BF16),
            pltpu.VMEM(spectral, BF16),
            pltpu.VMEM((Z - 1, *spectral), BF16),
            sem((BLOCKS // GROUP,)),
            sem((2,)),
            sem,
            sem,
            sem,
            sem((2, CHUNKS - min(JOINED) + 1)),
            sem,
            sem((2 * CHUNKS - 3,)),
            sem,
            sem((2,)),
            sem,
            sem,
            sem,
            sem((CHUNKS - 1,)),
            sem,
            sem,
            sem,
            sem,
            pltpu.SemaphoreType.REGULAR,
        ],
        compiler_params=pltpu.CompilerParams(
            collective_id=0, has_side_effects=True, vmem_limit_bytes=24 << 20
        ),
    )(*args)

    return pl.pallas_call(
        write,
        out_shape=jax.ShapeDtypeStruct((2, BLOCKS, COLS, COMP), F32),
        in_specs=[vmem_spec] * 3,
        out_specs=hbm_spec,
        scratch_shapes=[
            pltpu.VMEM((2, BLOCKS - early, COLS, COMP), F32),
            sem((CHUNKS,)),
        ],
        compiler_params=pltpu.CompilerParams(vmem_limit_bytes=16 << 20),
    )(*done)


def solution(mesh):
    in_specs = (
        P(None, "region", None, "eig"),
        P(None, "region", None, "eig"),
        P(None, "region", None, "eig"),
        P("eig"),
    )
    out_specs = P(None, "region", None, "eig")
    return jax.shard_map(shards, mesh=mesh, in_specs=in_specs, out_specs=out_specs, check_vma=False)
```
